32 devices in a mesh: attn: 4 (over y, core), expert: 4 (over z), loop: 2 (over x).
Axes of the slice: x: 2, y: 2, z: 4, core: 2. Of those that a mesh axis runs over, the one named last changes fastest.
Arguments:
- resid: bfloat16 [64, 3072], P(('expert', 'loop', 'attn')), may hold values from -33 to 33
- query: bfloat16 [64, 3072], P(('expert', 'loop', 'attn')), may hold values from -68.75573 to 68.75573
- key_cache: bfloat16 [64, 256, 512], P(('expert', 'loop', 'attn')), may hold values from -6 to 6
- value_cache: bfloat16 [64, 256, 512], P(('expert', 'loop', 'attn')), may hold values from -6 to 6
- new_key: bfloat16 [64, 512], P(('expert', 'loop', 'attn')), may hold values from -6 to 6
- new_value: bfloat16 [64, 512], P(('expert', 'loop', 'attn')), may hold values from -6 to 6
- cache_len: int32 [64], P(('expert', 'loop', 'attn')), may hold values from 2 to 256, as said below
- norm_gain: float32 [3072], replicated, may hold values from 0.5 to 1.5
- gate_weight: bfloat16 [4, 3072, 8192], P('expert', 'attn', 'loop'), may hold values from -0.109375 to 0.109375
- up_weight: bfloat16 [4, 3072, 8192], P('expert', 'attn', 'loop'), may hold values from -0.109375 to 0.109375
- down_weight: bfloat16 [4, 8192, 3072], P('expert', 'loop', 'attn'), may hold values from -0.0625 to 0.0625
- block_rows: int32 [4, 1, 128], P('expert'), may hold values from -1 to 63, as said below
- slot_weight: float32 [4, 1, 128], P('expert'), may hold values from 0.1 to 1
Outputs:
- layer_out: bfloat16 [64, 3072], P(('expert', 'loop', 'attn'))
The draws below stay inside these ranges and needn't reach their ends.
Inputs may be any that keep to these rules, and one draw needn't show every extreme that they name: `block_rows`: each of the 64 rows is named in the lists of exactly two different experts and nowhere else; within a list the rows ascend and fill the slots from the first one on; unused slots hold -1. One expert, drawn from the seed, is named by exactly 32 rows; the other experts by nearly equal numbers of rows. `cache_len`: some row uses all 256 positions.
All inputs are finite; a program needn't handle non-finite values.
Results may differ from the reference program's by a relative error of at most 0.0054.
Values may be sent and summed in bfloat16 or wider, within the bound.
A program may use at most 128 MiB of HBM per device.

```python
import math
import jax
import jax.numpy as jnp
from jax import lax

D = 3072
Q_HEADS = 24
KV_HEADS = 4
HEAD = 128
FF = 8192
BLOCK = 128
CACHE = 256
EXPERTS = 4
ROWS = 64
HOT = 32
CAP_BLOCKS = 1


def attention_keys(key):
    base_key = jax.random.fold_in(key, 23)
    key_main, key_query = jax.random.split(base_key)
    shape = (ROWS, CACHE, KV_HEADS * HEAD)
    cached = jnp.clip(jax.random.normal(key_main, shape, jnp.float32), -6.0, 6.0)
    return (cached, key_query)


def draw_key_cache(key, part):
    cached, key_query = attention_keys(key)
    return cached.astype(jnp.bfloat16)


def draw_query(key, part):
    cached, key_query = attention_keys(key)
    shape = (ROWS, Q_HEADS * HEAD)
    drawn = jnp.clip(jax.random.normal(key_query, shape, jnp.float32), -6.0, 6.0)
    return drawn.astype(jnp.bfloat16)


def draw_resid(key, part):
    base_key = jax.random.fold_in(key, 5)
    key_base, key_rows = jax.random.split(base_key, 2)
    row_scale = jnp.exp(jax.random.uniform(key_rows, (ROWS, 1), jnp.float32, math.log(0.32), math.log(3.2)))
    values = jnp.clip(jax.random.normal(key_base, (ROWS, D), jnp.float32), -6.0, 6.0) * row_scale
    return values.astype(jnp.bfloat16)


def draw_cache_len(key, part):
    lengths = jax.random.randint(jax.random.fold_in(key, 31), (ROWS,), 2, CACHE + 1)
    return lengths.at[0].set(CACHE).astype(jnp.int32)


def draw_block_rows(key, part):
    routing_key = jax.random.fold_in(key, 7)
    key_expert, key_row = jax.random.split(routing_key)
    expert_order = jax.random.permutation(key_expert, EXPERTS).astype(jnp.int32)
    hot_expert = expert_order[0]
    cold_experts = expert_order[1:]
    others = EXPERTS - 1
    row_order = jax.random.permutation(key_row, ROWS).astype(jnp.int32)
    position = jnp.arange(ROWS, dtype=jnp.int32)
    cold_place = jnp.maximum(position - HOT, 0)
    first_choice = jnp.where(position < HOT, hot_expert, cold_experts[cold_place % others])
    second_hot = cold_experts[position % others]
    second_cold = cold_experts[(cold_place + 1 + cold_place // others % (others - 1)) % others]
    second_choice = jnp.where(position < HOT, second_hot, second_cold)
    first_row = jnp.zeros((ROWS,), jnp.int32).at[row_order].set(first_choice)
    second_row = jnp.zeros((ROWS,), jnp.int32).at[row_order].set(second_choice)
    expert_ids = jnp.arange(EXPERTS, dtype=jnp.int32)[None, :]
    member = (first_row[:, None] == expert_ids) | (second_row[:, None] == expert_ids)
    member_count = member.astype(jnp.int32)
    list_rank = jnp.cumsum(member_count, axis=0) - 1
    list_slot = jnp.where(member, list_rank, CAP_BLOCKS * BLOCK)
    row_ids = jnp.broadcast_to(jnp.arange(ROWS, dtype=jnp.int32)[:, None], (ROWS, EXPERTS))
    column_ids = jnp.broadcast_to(expert_ids, (ROWS, EXPERTS))
    list_table = jnp.full((EXPERTS, CAP_BLOCKS * BLOCK), -1, jnp.int32)
    list_table = list_table.at[column_ids, list_slot].set(row_ids, mode='drop')
    return list_table.reshape(EXPERTS, CAP_BLOCKS, BLOCK)


def levels(rng, dims, shards, smallest, high):
    def one(dim, shards_of):
        heights = jax.random.uniform(jax.random.fold_in(jax.random.fold_in(rng, 6), dim), (shards_of,), jnp.float32, smallest / len(shards), high / len(shards))
        return jnp.repeat(jnp.exp(heights), dims[dim] // shards_of).reshape((-1,) + (1,) * (len(dims) - dim - 1))

    loudness = one(*shards[0])
    for cut in shards[1:]:
        loudness = loudness * one(*cut)
    return loudness


def gaussian(stream_key, dims, spread, most, pieces=(), kind=jnp.bfloat16):
    gain = levels(stream_key, dims, pieces, -0.22, 0.18) if pieces else 1.0
    drawn = jax.random.normal(stream_key, dims, jnp.float32) * spread * gain
    return jnp.minimum(jnp.maximum(drawn, -most), most).astype(kind)


def setup_inputs(seed: int = 0) -> dict:
    splits = jax.random.split(jax.random.key(seed), 14)
    resid = draw_resid(jax.random.fold_in(splits[13], 71), 0)
    query = draw_query(jax.random.fold_in(splits[13], 71), 0)
    key_cache = draw_key_cache(jax.random.fold_in(splits[13], 71), 0)
    value_cache = gaussian(splits[3], (ROWS, CACHE, KV_HEADS * HEAD), 1.0, 6.0, ((0, 32),))
    new_key = gaussian(splits[4], (ROWS, KV_HEADS * HEAD), 1.0, 6.0, ((0, 32),))
    new_value = gaussian(splits[5], (ROWS, KV_HEADS * HEAD), 1.0, 6.0, ((0, 32),))
    cache_len = draw_cache_len(jax.random.fold_in(splits[13], 71), 0)
    norm_gain = jnp.clip(jax.random.uniform(splits[7], (D,), jnp.float32, 0.5, 1.5), 0.5, 1.5)
    gate_weight = gaussian(splits[8], (EXPERTS, D, FF), D ** -0.5, 0.109375, ((0, 4), (1, 4), (2, 2)))
    up_weight = gaussian(splits[9], (EXPERTS, D, FF), D ** -0.5, 0.109375, ((0, 4), (1, 4), (2, 2)))
    down_weight = gaussian(splits[10], (EXPERTS, FF, D), FF ** -0.5, 0.0625, ((0, 4), (1, 2), (2, 4)))
    block_rows = draw_block_rows(jax.random.fold_in(splits[13], 71), 0)
    slot_weight = jnp.clip(0.1 + 0.9 * jax.random.uniform(splits[12], (EXPERTS, CAP_BLOCKS, BLOCK), jnp.float32) ** levels(splits[12], (EXPERTS, CAP_BLOCKS, BLOCK), ((0, 4),), -0.2, 0.2), 0.1, 1.0)
    return {"resid": resid, "query": query, "key_cache": key_cache, "value_cache": value_cache, "new_key": new_key, "new_value": new_value, "cache_len": cache_len, "norm_gain": norm_gain, "gate_weight": gate_weight, "up_weight": up_weight, "down_weight": down_weight, "block_rows": block_rows, "slot_weight": slot_weight}


def reference(resid, query, key_cache, value_cache, new_key, new_value, cache_len, norm_gain, gate_weight, up_weight, down_weight, block_rows, slot_weight):
    groups = Q_HEADS // KV_HEADS
    score_scale = HEAD ** (-0.5)
    highest = lax.Precision.HIGHEST

    def one_row(row_item):
        q_row, k_row, v_row, k_new, v_new, length = row_item
        queries = q_row.astype(jnp.float32).reshape(KV_HEADS, groups, HEAD)
        all_keys = jnp.concatenate([k_row, k_new[None, :]], axis=0).astype(jnp.float32).reshape(CACHE + 1, KV_HEADS, HEAD)
        all_values = jnp.concatenate([v_row, v_new[None, :]], axis=0).astype(jnp.float32).reshape(CACHE + 1, KV_HEADS, HEAD)
        scores = jnp.einsum('kgd,lkd->kgl', queries, all_keys, precision=highest) * score_scale
        position = jnp.arange(CACHE + 1)
        cache_live = (position < length) | (position == CACHE)
        scores = jnp.where(cache_live[None, None, :], scores, -jnp.inf)
        row_max = lax.optimization_barrier(jnp.max(scores, axis=-1, keepdims=True))
        exponent = jnp.exp(scores - row_max)
        softmax_weights = (exponent / lax.optimization_barrier(jnp.sum(exponent, axis=-1, keepdims=True))).astype(jnp.bfloat16)
        softmax_weights = lax.optimization_barrier(softmax_weights).astype(jnp.float32)
        attended = jnp.einsum('kgl,lkd->kgd', softmax_weights, all_values, precision=highest)
        return attended.reshape(Q_HEADS * HEAD)
    attended = lax.map(one_row, (query, key_cache, value_cache, new_key, new_value, cache_len))
    residual = (resid.astype(jnp.float32) + attended).astype(jnp.bfloat16)
    residual_wide = residual.astype(jnp.float32)
    normed = (residual_wide * lax.rsqrt(lax.optimization_barrier(jnp.mean(residual_wide * residual_wide, axis=-1, keepdims=True)) + 1e-05) * norm_gain).astype(jnp.bfloat16)
    slot_total = CAP_BLOCKS * BLOCK

    def one_expert(accumulated, expert_item):
        list_rows, weights, w_gate, w_up, w_down = expert_item
        slot_rows = list_rows.reshape(slot_total)
        slot_live = slot_rows >= 0
        picked = jnp.take(normed, jnp.where(slot_live, slot_rows, 0), axis=0)
        picked = jnp.where(slot_live[:, None], picked, jnp.zeros_like(picked))
        gate_total = jnp.dot(picked, w_gate, preferred_element_type=jnp.float32)
        up_total = jnp.dot(picked, w_up, preferred_element_type=jnp.float32)
        hidden = (jax.nn.silu(gate_total) * up_total).astype(jnp.bfloat16)
        expert_out = jnp.dot(hidden, w_down, preferred_element_type=jnp.float32)
        weighted = expert_out * jnp.where(slot_live, weights.reshape(slot_total), 0.0)[:, None]
        target = jnp.where(slot_live, slot_rows, ROWS)
        return (accumulated.at[target].add(weighted, mode='drop'), None)
    mixture, _ = lax.scan(one_expert, jnp.zeros((ROWS, D), jnp.float32), (block_rows, slot_weight, gate_weight, up_weight, down_weight))
    moe = lax.optimization_barrier(mixture.astype(jnp.bfloat16))
    return (residual.astype(jnp.float32) + moe.astype(jnp.float32)).astype(jnp.bfloat16)
```

```python
import functools

import jax
import jax.numpy as jnp
from jax import lax
from jax.experimental import pallas as pl
from jax.experimental.pallas import tpu as pltpu
from jax.sharding import PartitionSpec as P

Q_HEADS = 24
KV_HEADS = 4
HEAD = 128
MESH = pl.DeviceIdType.MESH
F32 = jnp.float32
BF16 = jnp.bfloat16


def kernel(
    sizes,
    len_ref,
    resid_ref,
    query_ref,
    nk_ref,
    nv_ref,
    gain_ref,
    list_ref,
    slotw_ref,
    kc_hbm,
    vc_hbm,
    wg_hbm,
    wu_hbm,
    wd_hbm,
    out_ref,
    kc,
    vc,
    wg,
    wu,
    wd,
    nb,
    xr,
    x32,
    ps,
    pr,
    cs,
    cr,
    hid,
    d32,
    ys,
    yr,
    kv_sem,
    w_sem,
    d_sem,
    x_send,
    x_recv,
    p_send,
    p_recv,
    c_send,
    c_recv,
    h_send,
    h_recv,
    f_send,
    f_recv,
    y_send,
    y_recv,
):
    n, experts, loops, cap = sizes
    total = n * experts * loops
    chips = n // 2
    here, width = resid_ref.shape
    cache = kc.shape[1]
    part = width // n
    quarter = wg.shape[2]
    rows = total * here
    slots = list_ref.shape[1]
    me_a = lax.axis_index("attn")
    me_e = lax.axis_index("expert")
    me_l = lax.axis_index("loop")
    me = (me_e * loops + me_l) * n + me_a
    core = lax.rem(me_a, 2)
    chip = lax.div(me_a, 2)
    partner = {"attn": chip * 2 + 1 - core, "expert": me_e, "loop": me_l}

    def place(index):
        group = lax.div(index, n)
        return {
            "attn": lax.rem(index, n),
            "expert": lax.div(group, loops),
            "loop": lax.rem(group, loops),
        }

    def side_of(shift, side):
        at = lax.rem(chip + shift + chips, chips)
        return at * 2 + (core if side else 1 - core)

    kv_copies = []
    for r in range(here):
        kv_copies.append(pltpu.make_async_copy(kc_hbm.at[r], kc.at[r], kv_sem.at[0, r]))
        kv_copies.append(pltpu.make_async_copy(vc_hbm.at[r], vc.at[r], kv_sem.at[1, r]))
    for copy in kv_copies:
        copy.start()

    barrier = pltpu.get_barrier_semaphore()

    def greet(d, carry):
        pl.semaphore_signal(
            barrier, inc=1, device_id=place(lax.rem(me + d, total)), device_id_type=MESH
        )
        return carry

    lax.fori_loop(1, total, greet, 0)

    shifts = list(range(1, chips)) + [0]
    w_copies = []
    for i, shift in enumerate(shifts):
        for side in range(2):
            k = 2 * i + side
            col = pl.multiple_of(side_of(shift, side) * quarter, quarter)
            pair = (
                pltpu.make_async_copy(wg_hbm.at[0, :, pl.ds(col, quarter)], wg.at[k], w_sem.at[0, k]),
                pltpu.make_async_copy(wu_hbm.at[0, :, pl.ds(col, quarter)], wu.at[k], w_sem.at[1, k]),
            )
            for copy in pair:
                copy.start()
            w_copies.append(pair)
    d_copies = []
    for shift in range(chips):
        for j in range(2):
            k = 2 * shift + j
            row = pl.multiple_of(side_of(-shift, 1 - j) * quarter, quarter)
            copy = pltpu.make_async_copy(wd_hbm.at[0, pl.ds(row, quarter), :], wd.at[k], d_sem.at[k])
            copy.start()
            d_copies.append(copy)

    rows_pad = max(rows, 128)
    slot_rows = list_ref[...]
    hot_t = jnp.where(
        lax.broadcasted_iota(jnp.int32, (rows_pad, slots), 0) == slot_rows, 1.0, 0.0
    ).astype(F32)
    hot = hot_t.T[:cap, :rows].astype(BF16)
    hot_t = hot_t[:rows]
    row_weight = jnp.sum(hot_t * slotw_ref[...], axis=1, keepdims=True)
    hot_t = hot_t.astype(BF16)

    groups = Q_HEADS // KV_HEADS
    scale = HEAD ** (-0.5)
    head_of = lax.broadcasted_iota(jnp.int32, (Q_HEADS, HEAD), 0) // groups
    position = lax.broadcasted_iota(jnp.int32, (Q_HEADS, cache), 1)
    queries = query_ref[...].astype(F32)
    new_keys = nk_ref[...].astype(F32)
    new_values = nv_ref[...].astype(F32)
    attended_rows = []
    for r in range(here):
        q24 = jnp.concatenate(
            [queries[r : r + 1, j * HEAD : (j + 1) * HEAD] for j in range(Q_HEADS)], axis=0
        )
        own_key = jnp.zeros((Q_HEADS, HEAD), F32)
        own_value = jnp.zeros((Q_HEADS, HEAD), F32)
        for g in range(KV_HEADS):
            lanes = slice(g * HEAD, (g + 1) * HEAD)
            own_key = jnp.where(head_of == g, new_keys[r : r + 1, lanes], own_key)
            own_value = jnp.where(head_of == g, new_values[r : r + 1, lanes], own_value)
        q_wide = jnp.concatenate(
            [jnp.where(head_of == g, q24, 0.0) for g in range(KV_HEADS)], axis=1
        ).astype(BF16)
        own_score = jnp.sum(q24 * own_key, axis=1, keepdims=True) * scale
        kv_copies[2 * r].wait()
        scores = (
            lax.dot_general(
                q_wide, kc[r], (((1,), (1,)), ((), ())), preferred_element_type=F32
            )
            * scale
        )
        scores = jnp.where(position < len_ref[r], scores, -jnp.inf)
        top = jnp.maximum(jnp.max(scores, axis=1, keepdims=True), own_score)
        exps = jnp.exp(scores - top)
        own_exp = jnp.exp(own_score - top)
        denominator = jnp.sum(exps, axis=1, keepdims=True) + own_exp
        probs = (exps / denominator).astype(BF16)
        own_prob = (own_exp / denominator).astype(BF16).astype(F32)
        kv_copies[2 * r + 1].wait()
        mixed = jnp.dot(probs, vc[r], preferred_element_type=F32)
        attended = own_prob * own_value
        for g in range(KV_HEADS):
            attended = attended + jnp.where(
                head_of == g, mixed[:, g * HEAD : (g + 1) * HEAD], 0.0
            )
        attended_rows.append(
            jnp.concatenate([attended[j : j + 1, :] for j in range(Q_HEADS)], axis=1)
        )
    attended = jnp.concatenate(attended_rows, axis=0)
    residual = (resid_ref[...].astype(F32) + attended).astype(BF16).astype(F32)
    normed = (
        residual
        * lax.rsqrt(jnp.mean(residual * residual, axis=-1, keepdims=True) + 1e-05)
        * gain_ref[...]
    ).astype(BF16)
    for a in range(n):
        nb[a] = normed[:, a * part : (a + 1) * part]

    pl.semaphore_wait(barrier, total - 1)

    def send_x(d, carry):
        to = lax.rem(me + d, total)
        pltpu.make_async_remote_copy(
            src_ref=nb.at[lax.rem(to, n)],
            dst_ref=xr.at[me],
            send_sem=x_send,
            recv_sem=x_recv,
            device_id=place(to),
            device_id_type=MESH,
        ).start()
        return carry

    lax.fori_loop(1, total, send_x, 0)
    xr[me] = nb[me_a]

    def wait_all(buffer, sem):
        block = buffer.at[pl.ds(0, total - 1)]
        pltpu.make_async_copy(block, block, sem).wait()

    wait_all(xr, x_recv)
    tiles = x32.shape[0]
    per_tile = x32.shape[1] // here

    def unpack(t, carry):
        for j in range(per_tile):
            x32[t, j * here : (j + 1) * here, :] = xr[t * per_tile + j].astype(F32)
        return carry

    lax.fori_loop(0, tiles, unpack, 0, unroll=min(8, tiles))
    every_row = x32[...].reshape(rows, part).astype(BF16)
    picked = jnp.dot(hot, every_row, preferred_element_type=F32).astype(BF16)

    def gate_up(k):
        for copy in w_copies[k]:
            copy.wait()
        gate = jnp.dot(picked, wg[k], preferred_element_type=F32)
        up = jnp.dot(picked, wu[k], preferred_element_type=F32)
        return jnp.concatenate([gate, up], axis=0)

    sends = []
    own = None
    for i, shift in enumerate(shifts):
        ps[i] = gate_up(2 * i).astype(BF16)
        to_partner = pltpu.make_async_remote_copy(
            src_ref=ps.at[i],
            dst_ref=pr.at[i],
            send_sem=p_send.at[i],
            recv_sem=p_recv.at[i],
            device_id=partner,
            device_id_type=MESH,
        )
        to_partner.start()
        sends.append(to_partner)
        own = gate_up(2 * i + 1)
        to_partner.wait_recv()
        own = own + pr[i].astype(F32)
        if shift:
            cs[shift - 1] = own.astype(BF16)
            across = pltpu.make_async_remote_copy(
                src_ref=cs.at[shift - 1],
                dst_ref=cr.at[shift - 1],
                send_sem=c_send.at[shift - 1],
                recv_sem=c_recv.at[shift - 1],
                device_id={"attn": side_of(shift, 1), "expert": me_e, "loop": me_l},
                device_id_type=MESH,
            )
            across.start()
            sends.append(across)
    for shift in range(1, chips):
        sends[2 * shift - 1].wait_recv()
        own = own + cr[shift - 1].astype(F32)
    gate = own[:cap]
    hid[0] = (gate / (1.0 + jnp.exp(-gate)) * own[cap:]).astype(BF16)

    across_h = []
    for shift in range(1, chips):
        copy = pltpu.make_async_remote_copy(
            src_ref=hid.at[0],
            dst_ref=hid.at[2 * shift],
            send_sem=h_send.at[shift],
            recv_sem=h_recv.at[shift],
            device_id={"attn": side_of(shift, 1), "expert": me_e, "loop": me_l},
            device_id_type=MESH,
        )
        copy.start()
        across_h.append(copy)

    def forward(shift):
        copy = pltpu.make_async_remote_copy(
            src_ref=hid.at[2 * shift],
            dst_ref=hid.at[2 * shift + 1],
            send_sem=f_send.at[shift],
            recv_sem=f_recv.at[shift],
            device_id=partner,
            device_id_type=MESH,
        )
        copy.start()
        return copy

    def down(k):
        d_copies[k].wait()
        return jnp.dot(hid[k], wd[k], preferred_element_type=F32)

    near = forward(0)
    expert_out = down(0)
    near.wait_recv()
    expert_out = expert_out + down(1)
    sends.append(near)
    for shift in range(1, chips):
        across_h[shift - 1].wait_recv()
        near = forward(shift)
        expert_out = expert_out + down(2 * shift)
        near.wait_recv()
        expert_out = expert_out + down(2 * shift + 1)
        sends.append(near)

    if slots > cap:
        expert_out = jnp.concatenate([expert_out, jnp.zeros((slots - cap, part), F32)], axis=0)
    high = expert_out.astype(BF16)
    low = (expert_out - high.astype(F32)).astype(BF16)
    dense = (
        jnp.dot(hot_t, high, preferred_element_type=F32)
        + jnp.dot(hot_t, low, preferred_element_type=F32)
    ) * row_weight
    d32[...] = dense.reshape(d32.shape)

    def pack(t, carry):
        for j in range(per_tile):
            ys[t * per_tile + j] = d32[t, j * here : (j + 1) * here, :].astype(BF16)
        return carry

    lax.fori_loop(0, tiles, pack, 0, unroll=min(8, tiles))

    def send_y(d, carry):
        to = lax.rem(me + d, total)
        pltpu.make_async_remote_copy(
            src_ref=ys.at[to],
            dst_ref=yr.at[me],
            send_sem=y_send,
            recv_sem=y_recv,
            device_id=place(to),
            device_id_type=MESH,
        ).start()
        return carry

    lax.fori_loop(1, total, send_y, 0)
    yr[me] = ys[me]
    wait_all(yr, y_recv)
    sources = total // n

    def add(g, sums):
        return tuple(sums[a] + yr[g * n + a].astype(F32) for a in range(n))

    sums = lax.fori_loop(
        0,
        sources,
        add,
        tuple(jnp.zeros((here, part), F32) for _ in range(n)),
        unroll=min(8, sources),
    )
    moe = jnp.concatenate(sums, axis=1).astype(BF16).astype(F32)
    out_ref[...] = (residual + moe).astype(BF16)

    for copy in sends + across_h:
        copy.wait_send()
    wait_all(xr, x_send)
    wait_all(yr, y_send)


def per_device(
    n,
    experts,
    loops,
    resid,
    query,
    key_cache,
    value_cache,
    new_key,
    new_value,
    cache_len,
    norm_gain,
    gate_weight,
    up_weight,
    down_weight,
    block_rows,
    slot_weight,
):
    here, width = resid.shape
    total = n * experts * loops
    chips = n // 2
    rows = here * total
    part = width // n
    quarter = gate_weight.shape[2] // n
    slots = block_rows.shape[1] * block_rows.shape[2]
    busiest = rows // 2
    shared = -(-(2 * rows - busiest) // (experts - 1))
    cap = min(slots, rows, (max(busiest, shared) // 8 + 1) * 8)
    cache, kv_width = key_cache.shape[1:]
    dma = pltpu.SemaphoreType.DMA
    vmem = pl.BlockSpec(memory_space=pltpu.VMEM)
    hbm = pl.BlockSpec(memory_space=pl.ANY)
    scratch = [
        pltpu.VMEM((here, cache, kv_width), BF16),
        pltpu.VMEM((here, cache, kv_width), BF16),
        pltpu.VMEM((n, part, quarter), BF16),
        pltpu.VMEM((n, part, quarter), BF16),
        pltpu.VMEM((n, quarter, part), BF16),
        pltpu.VMEM((n, here, part), BF16),
        pltpu.VMEM((total, here, part), BF16),
        pltpu.VMEM((rows // 8, 8, part), F32),
        pltpu.VMEM((chips, 2 * cap, quarter), BF16),
        pltpu.VMEM((chips, 2 * cap, quarter), BF16),
        pltpu.VMEM((chips - 1, 2 * cap, quarter), BF16),
        pltpu.VMEM((chips - 1, 2 * cap, quarter), BF16),
        pltpu.VMEM((n, cap, quarter), BF16),
        pltpu.VMEM((rows // 8, 8, part), F32),
        pltpu.VMEM((total, here, part), BF16),
        pltpu.VMEM((total, here, part), BF16),
        dma((2, here)),
        dma((2, n)),
        dma((n,)),
        dma,
        dma,
        dma((chips,)),
        dma((chips,)),
        dma((chips - 1,)),
        dma((chips - 1,)),
        dma((chips,)),
        dma((chips,)),
        dma((chips,)),
        dma((chips,)),
        dma,
        dma,
    ]
    return pl.pallas_call(
        functools.partial(kernel, (n, experts, loops, cap)),
        out_shape=jax.ShapeDtypeStruct((here, width), BF16),
        in_specs=[pl.BlockSpec(memory_space=pltpu.SMEM)] + [vmem] * 7 + [hbm] * 5,
        out_specs=vmem,
        scratch_shapes=scratch,
        compiler_params=pltpu.CompilerParams(
            collective_id=0, has_side_effects=True, vmem_limit_bytes=56 << 20
        ),
        name="moe_decode",
    )(
        cache_len,
        resid,
        query,
        new_key,
        new_value,
        norm_gain.reshape(1, width),
        block_rows.reshape(1, slots),
        slot_weight.reshape(1, slots),
        key_cache,
        value_cache,
        gate_weight,
        up_weight,
        down_weight,
    )


def solution(mesh):
    in_specs = (
        P(("expert", "loop", "attn"), None),
        P(("expert", "loop", "attn"), None),
        P(("expert", "loop", "attn"), None, None),
        P(("expert", "loop", "attn"), None, None),
        P(("expert", "loop", "attn"), None),
        P(("expert", "loop", "attn"), None),
        P(("expert", "loop", "attn")),
        P(),
        P("expert", "attn", "loop"),
        P("expert", "attn", "loop"),
        P("expert", "loop", "attn"),
        P("expert", None, None),
        P("expert", None, None),
    )
    out_specs = P(("expert", "loop", "attn"), None)
    body = functools.partial(
        per_device, mesh.shape["attn"], mesh.shape["expert"], mesh.shape["loop"]
    )
    return jax.shard_map(body, mesh=mesh, in_specs=in_specs, out_specs=out_specs, check_vma=False)
```

```python
import functools

import jax
import jax.numpy as jnp
from jax import lax
from jax.experimental import pallas as pl
from jax.experimental.pallas import tpu as pltpu
from jax.sharding import PartitionSpec as P

Q_HEADS = 24
KV_HEADS = 4
HEAD = 128
MESH = pl.DeviceIdType.MESH
F32 = jnp.float32
BF16 = jnp.bfloat16
CUTS = 2


def kernel(
    sizes,
    len_ref,
    resid_ref,
    query_ref,
    nk_ref,
    nv_ref,
    gain_ref,
    list_ref,
    slotw_ref,
    kc_hbm,
    vc_hbm,
    wg_hbm,
    wu_hbm,
    wd_hbm,
    out_ref,
    kc,
    vc,
    wg,
    wu,
    wd,
    nb,
    xr,
    x32,
    ps,
    pr,
    own,
    cs,
    cr,
    hid,
    d32,
    ys,
    yr,
    kv_sem,
    w_sem,
    d_sem,
    x_send,
    x_recv,
    p_send,
    p_recv,
    c_send,
    c_recv,
    h_send,
    h_recv,
    f_send,
    f_recv,
    y_send,
    y_recv,
):
    n, experts, loops, cap, cuts = sizes
    total = n * experts * loops
    chips = n // 2
    here, width = resid_ref.shape
    cache = kc.shape[1]
    part = width // n
    piece = wg.shape[2]
    quarter = piece * cuts
    rows = total * here
    slots = list_ref.shape[1]
    me_a = lax.axis_index("attn")
    me_e = lax.axis_index("expert")
    me_l = lax.axis_index("loop")
    me = (me_e * loops + me_l) * n + me_a
    core = lax.rem(me_a, 2)
    chip = lax.div(me_a, 2)
    partner = {"attn": chip * 2 + 1 - core, "expert": me_e, "loop": me_l}

    sources = total // n
    group = me_e * loops + me_l
    lanes_of = [lax.rem(me_a + d, n) for d in range(n)]

    def peers_of(d, first, act):
        other = lax.rem(group + d, sources)
        expert = lax.div(other, loops)
        loop = lax.rem(other, loops)
        for k in range(first, n):
            act(
                other * n + lanes_of[k],
                lanes_of[k],
                {"attn": lanes_of[k], "expert": expert, "loop": loop},
            )

    def each_peer(act):
        def step(d, carry):
            peers_of(d, 0, act)
            return carry

        lax.fori_loop(1, sources, step, 0, unroll=sources <= 8)
        peers_of(0, 1, act)

    def side_of(shift, side):
        at = lax.rem(chip + shift + chips, chips)
        return at * 2 + (core if side else 1 - core)

    kv_copies = []
    for r in range(here):
        kv_copies.append(pltpu.make_async_copy(kc_hbm.at[r], kc.at[r], kv_sem.at[0, r]))
        kv_copies.append(pltpu.make_async_copy(vc_hbm.at[r], vc.at[r], kv_sem.at[1, r]))
    for copy in kv_copies:
        copy.start()

    barrier = pltpu.get_barrier_semaphore()

    def greet(index, lane, device):
        pl.semaphore_signal(barrier, inc=1, device_id=device, device_id_type=MESH)

    each_peer(greet)

    shifts = list(range(1, chips)) + [0]
    w_copies = {}
    for shift in shifts:
        for side in range(2):
            for cut in range(cuts):
                k = len(w_copies)
                col = pl.multiple_of(side_of(shift, side) * quarter + cut * piece, piece)
                pair = (
                    pltpu.make_async_copy(
                        wg_hbm.at[0, :, pl.ds(col, piece)], wg.at[k], w_sem.at[0, k]
                    ),
                    pltpu.make_async_copy(
                        wu_hbm.at[0, :, pl.ds(col, piece)], wu.at[k], w_sem.at[1, k]
                    ),
                )
                for copy in pair:
                    copy.start()
                w_copies[shift, side, cut] = (k, pair)
    d_copies = []
    for shift in range(chips):
        for j in range(2):
            for cut in range(cuts):
                k = (2 * shift + j) * cuts + cut
                row = pl.multiple_of(side_of(-shift, 1 - j) * quarter + cut * piece, piece)
                copy = pltpu.make_async_copy(
                    wd_hbm.at[0, pl.ds(row, piece), :], wd.at[k], d_sem.at[k]
                )
                copy.start()
                d_copies.append(copy)

    rows_pad = max(rows, 128)
    slot_rows = list_ref[...]
    hot_t = jnp.where(
        lax.broadcasted_iota(jnp.int32, (rows_pad, slots), 0) == slot_rows, 1.0, 0.0
    ).astype(F32)
    hot = hot_t.T[:cap, :rows].astype(BF16)
    hot_t = hot_t[:rows]
    row_weight = jnp.sum(hot_t * slotw_ref[...], axis=1, keepdims=True)
    hot_t = hot_t.astype(BF16)

    groups = Q_HEADS // KV_HEADS
    scale = HEAD ** (-0.5)
    head_of = lax.broadcasted_iota(jnp.int32, (Q_HEADS, HEAD), 0) // groups
    position = lax.broadcasted_iota(jnp.int32, (Q_HEADS, cache), 1)
    queries = query_ref[...].astype(F32)
    new_keys = nk_ref[...].astype(F32)
    new_values = nv_ref[...].astype(F32)
    attended_rows = []
    for r in range(here):
        q24 = jnp.concatenate(
            [queries[r : r + 1, j * HEAD : (j + 1) * HEAD] for j in range(Q_HEADS)], axis=0
        )
        own_key = jnp.zeros((Q_HEADS, HEAD), F32)
        own_value = jnp.zeros((Q_HEADS, HEAD), F32)
        for g in range(KV_HEADS):
            lanes = slice(g * HEAD, (g + 1) * HEAD)
            own_key = jnp.where(head_of == g, new_keys[r : r + 1, lanes], own_key)
            own_value = jnp.where(head_of == g, new_values[r : r + 1, lanes], own_value)
        q_wide = jnp.concatenate(
            [jnp.where(head_of == g, q24, 0.0) for g in range(KV_HEADS)], axis=1
        ).astype(BF16)
        own_score = jnp.sum(q24 * own_key, axis=1, keepdims=True) * scale
        kv_copies[2 * r].wait()
        scores = (
            lax.dot_general(
                q_wide, kc[r], (((1,), (1,)), ((), ())), preferred_element_type=F32
            )
            * scale
        )
        scores = jnp.where(position < len_ref[r], scores, -jnp.inf)
        top = jnp.maximum(jnp.max(scores, axis=1, keepdims=True), own_score)
        exps = jnp.exp(scores - top)
        own_exp = jnp.exp(own_score - top)
        denominator = jnp.sum(exps, axis=1, keepdims=True) + own_exp
        probs = (exps / denominator).astype(BF16)
        own_prob = (own_exp / denominator).astype(BF16).astype(F32)
        kv_copies[2 * r + 1].wait()
        mixed = jnp.dot(probs, vc[r], preferred_element_type=F32)
        attended = own_prob * own_value
        for g in range(KV_HEADS):
            attended = attended + jnp.where(
                head_of == g, mixed[:, g * HEAD : (g + 1) * HEAD], 0.0
            )
        attended_rows.append(
            jnp.concatenate([attended[j : j + 1, :] for j in range(Q_HEADS)], axis=1)
        )
    attended = jnp.concatenate(attended_rows, axis=0)
    residual = (resid_ref[...].astype(F32) + attended).astype(BF16).astype(F32)
    normed = (
        residual
        * lax.rsqrt(jnp.mean(residual * residual, axis=-1, keepdims=True) + 1e-05)
        * gain_ref[...]
    ).astype(BF16)
    for a in range(n):
        nb[a] = normed[:, a * part : (a + 1) * part]

    pl.semaphore_wait(barrier, total - 1)

    def send_x(index, lane, device):
        pltpu.make_async_remote_copy(
            src_ref=nb.at[lane],
            dst_ref=xr.at[me],
            send_sem=x_send,
            recv_sem=x_recv,
            device_id=device,
            device_id_type=MESH,
        ).start()

    each_peer(send_x)
    xr[me] = nb[me_a]

    def wait_all(buffer, sem):
        block = buffer.at[pl.ds(0, total - 1)]
        pltpu.make_async_copy(block, block, sem).wait()

    wait_all(xr, x_recv)
    tiles = x32.shape[0]
    per_tile = x32.shape[1] // here

    def unpack(t, carry):
        for j in range(per_tile):
            x32[t, j * here : (j + 1) * here, :] = xr[t * per_tile + j].astype(F32)
        return carry

    lax.fori_loop(0, tiles, unpack, 0, unroll=min(8, tiles))
    every_row = x32[...].reshape(rows, part).astype(BF16)
    picked = jnp.dot(hot, every_row, preferred_element_type=F32).astype(BF16)

    sends = []

    def push(src_ref, dst_ref, send_sem, recv_sem, device):
        copy = pltpu.make_async_remote_copy(
            src_ref=src_ref,
            dst_ref=dst_ref,
            send_sem=send_sem,
            recv_sem=recv_sem,
            device_id=device,
            device_id_type=MESH,
        )
        copy.start()
        sends.append(copy)
        return copy

    def across(shift):
        return {"attn": side_of(shift, 1), "expert": me_e, "loop": me_l}

    def gate_up(shift, side, cut):
        k, pair = w_copies[shift, side, cut]
        for copy in pair:
            copy.wait()
        gate = jnp.dot(picked, wg[k], preferred_element_type=F32)
        up = jnp.dot(picked, wu[k], preferred_element_type=F32)
        return jnp.concatenate([gate, up], axis=0)

    def to_partner(shift):
        copies = []
        for cut in range(cuts):
            k = shift * cuts + cut
            ps[k] = gate_up(shift, 0, cut).astype(BF16)
            copies.append(push(ps.at[k], pr.at[k], p_send.at[k], p_recv.at[k], partner))
        return copies

    crossing = {}
    for shift in range(1, chips):
        near = to_partner(shift)
        for cut in range(cuts):
            k = (shift - 1) * cuts + cut
            both = gate_up(shift, 1, cut)
            near[cut].wait_recv()
            cs[k] = (both + pr[shift * cuts + cut].astype(F32)).astype(BF16)
            crossing[shift, cut] = push(
                cs.at[k], cr.at[k], c_send.at[k], c_recv.at[k], across(shift)
            )
    near = to_partner(0)
    for cut in range(cuts):
        own[cut] = gate_up(0, 1, cut)

    def down(k):
        d_copies[k].wait()
        return jnp.dot(hid[k], wd[k], preferred_element_type=F32)

    def spread(shift, cut):
        k = 2 * shift * cuts + cut
        return push(hid.at[k], hid.at[k + cuts], f_send.at[shift * cuts + cut],
                    f_recv.at[shift * cuts + cut], partner)

    expert_out = jnp.zeros((cap, part), F32)
    far, beside = {}, {}
    for cut in range(cuts):
        near[cut].wait_recv()
        both = own[cut] + pr[cut].astype(F32)
        for shift in range(1, chips):
            crossing[shift, cut].wait_recv()
            both = both + cr[(shift - 1) * cuts + cut].astype(F32)
        gate = both[:cap]
        hid[cut] = (gate / (1.0 + jnp.exp(-gate)) * both[cap:]).astype(BF16)
        for shift in range(1, chips):
            k = shift * cuts + cut
            far[shift, cut] = push(
                hid.at[cut], hid.at[2 * shift * cuts + cut], h_send.at[k], h_recv.at[k], across(shift)
            )
        beside[0, cut] = spread(0, cut)
        expert_out = expert_out + down(cut)
    for cut in range(cuts):
        beside[0, cut].wait_recv()
        expert_out = expert_out + down(cuts + cut)
    for shift in range(1, chips):
        for cut in range(cuts):
            far[shift, cut].wait_recv()
            beside[shift, cut] = spread(shift, cut)
            expert_out = expert_out + down(2 * shift * cuts + cut)
    for shift in range(1, chips):
        for cut in range(cuts):
            beside[shift, cut].wait_recv()
            expert_out = expert_out + down((2 * shift + 1) * cuts + cut)

    if slots > cap:
        expert_out = jnp.concatenate([expert_out, jnp.zeros((slots - cap, part), F32)], axis=0)
    high = expert_out.astype(BF16)
    low = (expert_out - high.astype(F32)).astype(BF16)
    dense = (
        jnp.dot(hot_t, high, preferred_element_type=F32)
        + jnp.dot(hot_t, low, preferred_element_type=F32)
    ) * row_weight
    d32[...] = dense.reshape(d32.shape)

    def pack(t, carry):
        for j in range(per_tile):
            ys[t * per_tile + j] = d32[t, j * here : (j + 1) * here, :].astype(BF16)
        return carry

    lax.fori_loop(0, tiles, pack, 0, unroll=min(8, tiles))

    def send_y(index, lane, device):
        pltpu.make_async_remote_copy(
            src_ref=ys.at[index],
            dst_ref=yr.at[me],
            send_sem=y_send,
            recv_sem=y_recv,
            device_id=device,
            device_id_type=MESH,
        ).start()

    each_peer(send_y)
    yr[me] = ys[me]
    wait_all(yr, y_recv)
    def add(g, sums):
        return tuple(sums[a] + yr[g * n + a].astype(F32) for a in range(n))

    sums = lax.fori_loop(
        0,
        sources,
        add,
        tuple(jnp.zeros((here, part), F32) for _ in range(n)),
        unroll=min(8, sources),
    )
    moe = jnp.concatenate(sums, axis=1).astype(BF16).astype(F32)
    out_ref[...] = (residual + moe).astype(BF16)

    for copy in sends:
        copy.wait_send()
    wait_all(xr, x_send)
    wait_all(yr, y_send)


def per_device(
    n,
    experts,
    loops,
    resid,
    query,
    key_cache,
    value_cache,
    new_key,
    new_value,
    cache_len,
    norm_gain,
    gate_weight,
    up_weight,
    down_weight,
    block_rows,
    slot_weight,
):
    here, width = resid.shape
    total = n * experts * loops
    chips = n // 2
    rows = here * total
    part = width // n
    quarter = gate_weight.shape[2] // n
    cuts = CUTS if quarter % (128 * CUTS) == 0 else 1
    piece = quarter // cuts
    slots = block_rows.shape[1] * block_rows.shape[2]
    busiest = rows // 2
    shared = -(-(2 * rows - busiest) // (experts - 1))
    cap = min(slots, rows, (max(busiest, shared) // 8 + 1) * 8)
    cache, kv_width = key_cache.shape[1:]
    dma = pltpu.SemaphoreType.DMA
    vmem = pl.BlockSpec(memory_space=pltpu.VMEM)
    hbm = pl.BlockSpec(memory_space=pl.ANY)
    scratch = [
        pltpu.VMEM((here, cache, kv_width), BF16),
        pltpu.VMEM((here, cache, kv_width), BF16),
        pltpu.VMEM((n * cuts, part, piece), BF16),
        pltpu.VMEM((n * cuts, part, piece), BF16),
        pltpu.VMEM((n * cuts, piece, part), BF16),
        pltpu.VMEM((n, here, part), BF16),
        pltpu.VMEM((total, here, part), BF16),
        pltpu.VMEM((rows // 8, 8, part), F32),
        pltpu.VMEM((chips * cuts, 2 * cap, piece), BF16),
        pltpu.VMEM((chips * cuts, 2 * cap, piece), BF16),
        pltpu.VMEM((cuts, 2 * cap, piece), F32),
        pltpu.VMEM(((chips - 1) * cuts, 2 * cap, piece), BF16),
        pltpu.VMEM(((chips - 1) * cuts, 2 * cap, piece), BF16),
        pltpu.VMEM((n * cuts, cap, piece), BF16),
        pltpu.VMEM((rows // 8, 8, part), F32),
        pltpu.VMEM((total, here, part), BF16),
        pltpu.VMEM((total, here, part), BF16),
        dma((2, here)),
        dma((2, n * cuts)),
        dma((n * cuts,)),
        dma,
        dma,
        dma((chips * cuts,)),
        dma((chips * cuts,)),
        dma(((chips - 1) * cuts,)),
        dma(((chips - 1) * cuts,)),
        dma((chips * cuts,)),
        dma((chips * cuts,)),
        dma((chips * cuts,)),
        dma((chips * cuts,)),
        dma,
        dma,
    ]
    return pl.pallas_call(
        functools.partial(kernel, (n, experts, loops, cap, cuts)),
        out_shape=jax.ShapeDtypeStruct((here, width), BF16),
        in_specs=[pl.BlockSpec(memory_space=pltpu.SMEM)] + [vmem] * 7 + [hbm] * 5,
        out_specs=vmem,
        scratch_shapes=scratch,
        compiler_params=pltpu.CompilerParams(
            collective_id=0, has_side_effects=True, vmem_limit_bytes=56 << 20
        ),
        name="moe_decode",
    )(
        cache_len,
        resid,
        query,
        new_key,
        new_value,
        norm_gain.reshape(1, width),
        block_rows.reshape(1, slots),
        slot_weight.reshape(1, slots),
        key_cache,
        value_cache,
        gate_weight,
        up_weight,
        down_weight,
    )


def solution(mesh):
    in_specs = (
        P(("expert", "loop", "attn"), None),
        P(("expert", "loop", "attn"), None),
        P(("expert", "loop", "attn"), None, None),
        P(("expert", "loop", "attn"), None, None),
        P(("expert", "loop", "attn"), None),
        P(("expert", "loop", "attn"), None),
        P(("expert", "loop", "attn")),
        P(),
        P("expert", "attn", "loop"),
        P("expert", "attn", "loop"),
        P("expert", "loop", "attn"),
        P("expert", None, None),
        P("expert", None, None),
    )
    out_specs = P(("expert", "loop", "attn"), None)
    body = functools.partial(
        per_device, mesh.shape["attn"], mesh.shape["expert"], mesh.shape["loop"]
    )
    return jax.shard_map(body, mesh=mesh, in_specs=in_specs, out_specs=out_specs, check_vma=False)
```
